32 devices in a mesh: pole: 2 (over x), row: 8 (over z, y), col: 2 (over core).
Axes of the slice: x: 2, y: 2, z: 4, core: 2. Of those that a mesh axis runs over, the one named last changes fastest.
Arguments:
- ancestor_inverse: float32 [2, 24576, 12288], P(None, ('pole', 'row'), 'col'), parts along dimension 1, may hold values from -6 to 6
- factor_panels: float32 [4, 2, 24576, 128], P(None, None, ('pole', 'col', 'row')), parts along dimension 2, may hold values from -0.0546875 to 0.0546875
- diag_inverse: float32 [8, 2, 128, 128], P('pole'), parts along dimension 0, may hold values from -6 to 6
- coupling: float32 [4, 2, 128, 128], P('pole'), parts along dimension 0, may hold values from -0.5 to 0.5
- block_pattern: int32 [4, 96], replicated, may hold values from 0 to 1, as said below
- tree_order: int32 [4], replicated, may hold values from 0 to 3, each once
Outputs:
- inverse_panels: float32 [4, 2, 24576, 128], P(None, None, ('pole', 'row')), parts along dimension 2
- inverse_diagonal: float32 [8, 2, 128, 128], P('pole'), parts along dimension 0
- inverse_coupling: float32 [4, 2, 128, 128], P('pole'), parts along dimension 0
The draws below stay inside these ranges and needn't reach their ends.
There are 2 independent parts, one for each index of `pole`. The reference program is written for one: setup_inputs(seed, part) draws one part's arguments, and reference() takes and returns one part's arrays. A program takes and returns all parts, laid end to end along the dimension named above; an argument that names none is the same for every part. Nothing has to cross between parts.
Inputs may be any that keep to these rules, and one draw needn't show every extreme that they name: `tree_order`: each supernode number appears once. `block_pattern`: blocks 0 and 48 lie in every supernode's structure.
All inputs are finite; a program needn't handle non-finite values.
Results may differ from the reference program's by a relative error of at most 0.0001.
Values sent between devices are 32-bit elements; how exact they have to be, the bound alone decides.
A program may use at most 192 MiB of HBM per device.

```python
import jax
import jax.numpy as jnp
from jax import lax

B = 128
ANC = 12288
SUPER = 4
NB = 96


def draw_block_pattern(key, part):
    random_level = jax.random.randint(key, (SUPER, NB), 0, 8)
    pattern_live = (random_level < 5).astype(jnp.int32)
    block_index = jnp.arange(NB, dtype=jnp.int32)
    forced_blocks = ((block_index == 0) | (block_index == NB // 2)).astype(jnp.int32)
    return jnp.maximum(pattern_live, forced_blocks[None, :])


def block_levels(rng, extent, cuts, least, high):
    loudness, own = 1.0, jax.random.fold_in(rng, 6)
    for axis_at, shards_of in cuts:
        draws = jnp.exp(jax.random.uniform(jax.random.fold_in(own, axis_at), (shards_of,), jnp.float32, least / len(cuts), high / len(cuts)))
        loudness = loudness * jnp.repeat(draws, extent[axis_at] // shards_of).reshape([-1 if axis == axis_at else 1 for axis in range(len(extent))])
    return loudness


def normal_values(key, shape, width, reach, shards=(), kind=jnp.bfloat16):
    gain = block_levels(key, shape, shards, -0.22, 0.18) if shards else 1.0
    array = jax.random.normal(key, shape, jnp.float32) * width * gain
    return jnp.minimum(jnp.maximum(array, -reach), reach).astype(kind)


def setup_inputs(seed: int = 0, part: int = 0) -> dict:
    splits = jax.random.split(jax.random.key(seed), 7)
    part_splits = jax.random.split(jax.random.fold_in(splits[6], part), 7)
    ancestor_inverse = normal_values(part_splits[0], (2, ANC, ANC), 1.0, 6.0, ((1, 8), (2, 2)), jnp.float32)
    factor_panels = normal_values(part_splits[1], (SUPER, 2, ANC, B), ANC ** -0.5, 0.0546875, ((2, 16),), jnp.float32)
    diag_inverse = normal_values(part_splits[2], (SUPER, 2, B, B), 1.0, 6.0, (), jnp.float32)
    coupling = normal_values(part_splits[3], (SUPER // 2, 2, B, B), B ** -0.5, 0.5, (), jnp.float32)
    block_pattern = draw_block_pattern(jax.random.fold_in(splits[6], 71), part)
    tree_order = jax.random.permutation(splits[5], SUPER).astype(jnp.int32)
    return {"ancestor_inverse": ancestor_inverse, "factor_panels": factor_panels, "diag_inverse": diag_inverse, "coupling": coupling, "block_pattern": block_pattern, "tree_order": tree_order}


def matmul(left_side, right_side):
    return jnp.dot(left_side, right_side, preferred_element_type=jnp.float32, precision=lax.Precision.HIGHEST)


def multiply(left_side, right_side):
    real_part = matmul(left_side[0], right_side[0]) - matmul(left_side[1], right_side[1])
    imag_part = matmul(left_side[0], right_side[1]) + matmul(left_side[1], right_side[0])
    return jnp.stack([real_part, imag_part])


def flipped(matrix):
    return jnp.swapaxes(matrix, 1, 2)


def reference(ancestor_inverse, factor_panels, diag_inverse, coupling, block_pattern, tree_order):
    row_masks = jnp.repeat(block_pattern.astype(jnp.float32), B, axis=1)
    sorted_masks = jnp.take(row_masks, tree_order, axis=0)
    masks = jnp.concatenate([sorted_masks[:2], sorted_masks[2:] * sorted_masks[:2]], axis=0)
    panels = jnp.take(factor_panels, tree_order, axis=0) * masks[:, None, :, None]
    diag_blocks = jnp.take(diag_inverse, tree_order, axis=0)
    parent_cols = []
    parent_diag = []
    for tree_slot in range(2):
        column_block = -masks[tree_slot][None, :, None] * multiply(ancestor_inverse, panels[tree_slot])
        parent_cols.append(column_block)
        parent_diag.append(diag_blocks[tree_slot] - multiply(flipped(panels[tree_slot]), column_block))
    child_cols = []
    child_diag = []
    crosses = []
    for tree_slot in range(2):
        child_slot = tree_slot + 2
        link_block = coupling[tree_slot]
        column_block = -masks[child_slot][None, :, None] * (
            multiply(ancestor_inverse, panels[child_slot]) + multiply(parent_cols[tree_slot], link_block))
        cross_block = -(multiply(flipped(parent_cols[tree_slot]), panels[child_slot])
                        + multiply(parent_diag[tree_slot], link_block))
        child_cols.append(column_block)
        crosses.append(cross_block)
        child_diag.append(diag_blocks[child_slot] - multiply(flipped(panels[child_slot]), column_block)
                          - multiply(flipped(link_block), cross_block))
    all_cols = jnp.stack(parent_cols + child_cols)
    all_diag = jnp.stack(parent_diag + child_diag)
    inverse_panels = jnp.zeros_like(factor_panels).at[tree_order].set(all_cols)
    inverse_diagonal = jnp.zeros_like(diag_inverse).at[tree_order].set(all_diag)
    return inverse_panels, inverse_diagonal, jnp.stack(crosses)
```

```python
import functools
import math

import jax
import jax.numpy as jnp
from jax import lax
from jax.experimental import pallas as pl
from jax.experimental.pallas import tpu as pltpu
from jax.sharding import PartitionSpec as P

BF16 = jnp.bfloat16
F32 = jnp.float32
GROUP = 4
VMEM_BYTES = 64 * 1024 * 1024 - 256 * 1024


def swapped(block, axis, bit):
    count = lax.axis_size(axis)
    route = []
    for low in range(count):
        high = low | 1 << bit
        if high != low and high < count:
            route += [(low, high), (high, low)]
    return lax.ppermute(block, axis, route)


def matmul(left_side, right_side):
    return jnp.dot(
        left_side, right_side, preferred_element_type=jnp.float32, precision=lax.Precision.HIGHEST
    )


def multiply(left_side, right_side):
    real_part = matmul(left_side[0], right_side[0]) - matmul(left_side[1], right_side[1])
    imag_part = matmul(left_side[0], right_side[1]) + matmul(left_side[1], right_side[0])
    return jnp.stack([real_part, imag_part])


def flipped(matrix):
    return jnp.swapaxes(matrix, 1, 2)


def row_masks(pattern_eff, first_row, row_count, block_rows):
    row_index = first_row + jnp.arange(row_count, dtype=jnp.int32)
    blocks = row_index // block_rows
    onehot = (blocks[:, None] == jnp.arange(pattern_eff.shape[1], dtype=jnp.int32)[None, :]).astype(
        jnp.float32
    )
    return matmul(pattern_eff, onehot.T)


def per_device_dense(ancestor_inverse, factor_panels, diag_inverse, coupling, block_pattern, tree_order):
    grid_row = lax.axis_index("row")
    grid_col = lax.axis_index("col")
    tile_rows = ancestor_inverse.shape[1]
    half_rows = ancestor_inverse.shape[2]
    piece_rows = factor_panels.shape[2]
    block_rows = factor_panels.shape[3]
    super_count = factor_panels.shape[0]
    share_rows = tile_rows // 2
    sorted_pattern = jnp.take(block_pattern, tree_order, axis=0).astype(jnp.float32)
    pattern_eff = jnp.concatenate(
        [sorted_pattern[:2], sorted_pattern[2:] * sorted_pattern[:2]], axis=0
    )
    source_mask = row_masks(
        pattern_eff, grid_col * half_rows + grid_row * piece_rows, piece_rows, block_rows
    )
    target_mask = row_masks(pattern_eff, grid_row * tile_rows, tile_rows, block_rows)
    panels = jnp.take(factor_panels, tree_order, axis=0) * source_mask[:, None, :, None]
    diag_blocks = jnp.take(diag_inverse, tree_order, axis=0)
    columns = []
    products = []
    for tree_slot in range(super_count):
        gathered = lax.all_gather(panels[tree_slot], "row", axis=1, tiled=True)
        columns.append(gathered)
        products.append(lax.psum(multiply(ancestor_inverse, gathered), "col"))
    own_flag = (grid_row * tile_rows // half_rows == grid_col).astype(jnp.float32)
    offset = jnp.clip(grid_row * tile_rows - grid_col * half_rows, 0, half_rows - tile_rows)
    own_windows = jnp.stack(
        [
            lax.dynamic_slice_in_dim(column_set, offset, tile_rows, 1) * own_flag
            for column_set in columns
        ]
    )
    partner_windows = swapped(own_windows, "col", 0)
    tile_windows = own_windows + partner_windows

    def share(matrix):
        return lax.dynamic_slice_in_dim(matrix, grid_col * share_rows, share_rows, 1)

    windows = [share(tile_windows[tree_slot]) for tree_slot in range(super_count)]
    parent_cols = [
        -target_mask[tree_slot][None, :, None] * products[tree_slot] for tree_slot in range(2)
    ]
    child_cols = [
        -target_mask[tree_slot + 2][None, :, None]
        * (products[tree_slot + 2] + multiply(parent_cols[tree_slot], coupling[tree_slot]))
        for tree_slot in range(2)
    ]
    parent_local = [
        multiply(flipped(windows[tree_slot]), share(parent_cols[tree_slot]))
        for tree_slot in range(2)
    ]
    cross_local = [
        multiply(flipped(share(parent_cols[tree_slot])), windows[tree_slot + 2])
        for tree_slot in range(2)
    ]
    child_local = [
        multiply(flipped(windows[tree_slot + 2]), share(child_cols[tree_slot]))
        for tree_slot in range(2)
    ]
    parent_sums = lax.psum(jnp.stack(parent_local), ("row", "col"))
    parent_diag = [diag_blocks[tree_slot] - parent_sums[tree_slot] for tree_slot in range(2)]
    child_totals = lax.psum(jnp.stack(cross_local + child_local), ("row", "col"))
    crosses = [
        -(child_totals[tree_slot] + multiply(parent_diag[tree_slot], coupling[tree_slot]))
        for tree_slot in range(2)
    ]
    child_sums = [child_totals[2 + tree_slot] for tree_slot in range(2)]
    child_diag = [
        diag_blocks[tree_slot + 2]
        - child_sums[tree_slot]
        - multiply(flipped(coupling[tree_slot]), crosses[tree_slot])
        for tree_slot in range(2)
    ]
    all_cols = jnp.stack(parent_cols + child_cols)
    all_diag = jnp.stack(parent_diag + child_diag)
    inverse_panels = jnp.zeros_like(all_cols).at[tree_order].set(all_cols)
    inverse_diagonal = jnp.zeros_like(all_diag).at[tree_order].set(all_diag)
    return (inverse_panels, inverse_diagonal, jnp.stack(crosses))


def halves(value):
    high = value.astype(BF16)
    return high, (value - high.astype(F32)).astype(BF16)


def pack_kernel(source_ref, panel_ref, packed_ref):
    packed_ref[0] = panel_ref[0].reshape(packed_ref.shape[1:])


def pack(factor_panels, supernode, block, count, size):
    source = jnp.stack([supernode[:count], block[:count]])
    return pl.pallas_call(
        pack_kernel,
        out_shape=jax.ShapeDtypeStruct((count, 2 * size, size), F32),
        grid_spec=pltpu.PrefetchScalarGridSpec(
            num_scalar_prefetch=1,
            grid=(count,),
            in_specs=[
                pl.BlockSpec((1, 2, size, size), lambda g, source: (source[0, g], 0, source[1, g], 0))
            ],
            out_specs=pl.BlockSpec((1, 2 * size, size), lambda g, source: (g, 0, 0)),
        ),
    )(source, factor_panels)


def product_kernel(
    sources, per_source, size, steps_k,
    counts_ref, k_list_ref, place_ref, k_count_ref, row_live_ref, k_any_ref,
    panel_ref, a_ref, out_ref,
    b_high, b_low, a_high, a_low, acc,
):
    step = pl.program_id(0)

    @pl.when(step == 0)
    def _():
        b_high[sources * per_source] = jnp.zeros(b_high.shape[1:], BF16)
        b_low[sources * per_source] = jnp.zeros(b_low.shape[1:], BF16)

    @pl.when(step < sources)
    def _():
        @pl.loop(0, counts_ref[step])
        def _(at):
            block = panel_ref[0, at]
            high, low = halves(jnp.concatenate([block[:size], block[size:]], axis=1))
            b_high[step * per_source + at] = high
            b_low[step * per_source + at] = low

    @pl.when(step >= sources)
    def _():
        row = step - sources
        live = [row_live_ref[slot, row] for slot in range(4)]

        @pl.when(live[0] + live[1] + live[2] + live[3] > 0)
        def _():
            @pl.loop(0, steps_k)
            def _(k):
                @pl.when(k_any_ref[k] > 0)
                def _():
                    columns = pl.ds(pl.multiple_of(k * size, size), size)
                    for part in range(2):
                        high, low = halves(a_ref[part, :, columns])
                        a_high[k, part * size:(part + 1) * size] = high
                        a_low[k, part * size:(part + 1) * size] = low

        for slot in range(4):
            @pl.when(live[slot] == 0)
            def _():
                out_ref[slot] = jnp.zeros(out_ref.shape[1:], F32)

            @pl.when(live[slot] > 0)
            def _():
                acc[...] = jnp.zeros_like(acc)

                @pl.loop(0, k_count_ref[slot])
                def _(group):
                    left, right = [], []
                    for member in range(GROUP):
                        k = k_list_ref[slot, group * GROUP + member]
                        place = place_ref[slot, group * GROUP + member]
                        left += [a_high[k], a_low[k], a_high[k]]
                        right += [b_high[place], b_high[place], b_low[place]]
                    acc[...] += jnp.dot(
                        jnp.concatenate(left, axis=1),
                        jnp.concatenate(right, axis=0),
                        preferred_element_type=F32,
                    )

                out_ref[slot, 0] = acc[:size, :size] - acc[size:, size:]
                out_ref[slot, 1] = acc[:size, size:] + acc[size:, :size]


def products_of(ancestor_inverse, gathered, counts, k_list, place, k_count, row_live, k_any, size):
    sources, per_source = gathered.shape[:2]
    tile_rows, half_rows = ancestor_inverse.shape[1:]
    steps_k = half_rows // size
    rows = tile_rows // size
    return pl.pallas_call(
        functools.partial(product_kernel, sources, per_source, size, steps_k),
        out_shape=jax.ShapeDtypeStruct((4, 2, tile_rows, size), F32),
        grid_spec=pltpu.PrefetchScalarGridSpec(
            num_scalar_prefetch=6,
            grid=(sources + rows,),
            in_specs=[
                pl.BlockSpec(
                    (1, per_source, 2 * size, size),
                    lambda g, *_: (jnp.minimum(g, sources - 1), 0, 0, 0),
                ),
                pl.BlockSpec(
                    (2, size, half_rows), lambda g, *_: (0, jnp.maximum(g - sources, 0), 0)
                ),
            ],
            out_specs=pl.BlockSpec(
                (4, 2, size, size), lambda g, *_: (0, 0, jnp.maximum(g - sources, 0), 0)
            ),
            scratch_shapes=[
                pltpu.VMEM((sources * per_source + 1, size, 2 * size), BF16),
                pltpu.VMEM((sources * per_source + 1, size, 2 * size), BF16),
                pltpu.VMEM((steps_k, 2 * size, size), BF16),
                pltpu.VMEM((steps_k, 2 * size, size), BF16),
                pltpu.VMEM((2 * size, 2 * size), F32),
            ],
        ),
        compiler_params=pltpu.CompilerParams(vmem_limit_bytes=VMEM_BYTES),
    )(counts, k_list, place, k_count, row_live, k_any, gathered, ancestor_inverse)


def wide(matrix):
    return jnp.concatenate([matrix[0], matrix[1]], axis=1)


def folded(product, size, transposed):
    return jnp.stack(
        [
            product[:size, :size] - product[size:, size:],
            product[:size, size:] + product[size:, :size],
        ]
    )


def contracted(left_side, right_side):
    return lax.dot_general(
        left_side, right_side, (((0,), (0,)), ((), ())),
        preferred_element_type=F32, precision=lax.Precision.HIGHEST,
    )


def finish_kernel(
    size, live_ref, own_ref, order_ref, source_ref,
    mine_ref, other_ref, link_ref, w0_ref, w1_ref, w2_ref, w3_ref,
    columns_ref, sums_ref,
):
    row = pl.program_id(0)
    windows = (w0_ref, w1_ref, w2_ref, w3_ref)

    @pl.when(row == 0)
    def _():
        sums_ref[...] = jnp.zeros_like(sums_ref)

    def window(slot):
        block = windows[slot][0, 0]
        return jnp.concatenate([block[:size], block[size:]], axis=1)

    for tree in range(2):
        child = tree + 2
        parent_at = order_ref[tree]
        child_at = order_ref[child]

        @pl.when(live_ref[tree, row] == 0)
        def _():
            columns_ref[parent_at] = jnp.zeros(columns_ref.shape[1:], F32)

        @pl.when(live_ref[child, row] == 0)
        def _():
            columns_ref[child_at] = jnp.zeros(columns_ref.shape[1:], F32)

        @pl.when(live_ref[tree, row] > 0)
        def _():
            columns_ref[parent_at] = -(mine_ref[tree] + other_ref[tree])

            @pl.when(own_ref[row] > 0)
            def _():
                sums_ref[tree] += folded(
                    contracted(window(tree), wide(columns_ref[parent_at])), size, True
                )

        @pl.when(live_ref[child, row] > 0)
        def _():
            parent = columns_ref[parent_at]
            linked = folded(
                matmul(jnp.concatenate([parent[0], parent[1]], axis=0), wide(link_ref[tree])),
                size, False,
            )
            columns_ref[child_at] = -(mine_ref[child] + other_ref[child] + linked)

            @pl.when(own_ref[row] > 0)
            def _():
                other_window = window(child)
                sums_ref[child] += folded(
                    contracted(wide(parent), other_window), size, True
                )
                sums_ref[tree + 4] += folded(
                    contracted(other_window, wide(columns_ref[child_at])), size, True
                )


def finish(mine, other, coupling, gathered, live, own, tree_order, source, size):
    rows = live.shape[1]

    def window_map(slot, g, live, own, order, source):
        return (source[0, slot, g], source[1, slot, g], 0, 0)

    return pl.pallas_call(
        functools.partial(finish_kernel, size),
        out_shape=(
            jax.ShapeDtypeStruct(mine.shape, F32),
            jax.ShapeDtypeStruct((6, 2, size, size), F32),
        ),
        grid_spec=pltpu.PrefetchScalarGridSpec(
            num_scalar_prefetch=4,
            grid=(rows,),
            in_specs=[
                pl.BlockSpec((4, 2, size, size), lambda g, *_: (0, 0, g, 0)),
                pl.BlockSpec((4, 2, size, size), lambda g, *_: (0, 0, g, 0)),
                pl.BlockSpec(coupling.shape, lambda g, *_: (0, 0, 0, 0)),
            ]
            + [
                pl.BlockSpec((1, 1, 2 * size, size), functools.partial(window_map, slot))
                for slot in range(4)
            ],
            out_specs=(
                pl.BlockSpec((4, 2, size, size), lambda g, *_: (0, 0, g, 0)),
                pl.BlockSpec((6, 2, size, size), lambda g, *_: (0, 0, 0, 0)),
            ),
        ),
        compiler_params=pltpu.CompilerParams(vmem_limit_bytes=VMEM_BYTES),
    )(live, own, tree_order, source, mine, other, coupling, gathered, gathered, gathered, gathered)


def gather_rows(packed, branch):
    return lax.all_gather(packed, "row", axis=0, tiled=False)


def per_device_blocks(
    ancestor_inverse, factor_panels, diag_inverse, coupling, block_pattern, tree_order
):
    grid_row = lax.axis_index("row")
    grid_col = lax.axis_index("col")
    row_count = lax.axis_size("row")
    col_count = lax.axis_size("col")
    size = factor_panels.shape[3]
    tile_blocks = ancestor_inverse.shape[1] // size
    half_blocks = ancestor_inverse.shape[2] // size
    piece_blocks = factor_panels.shape[2] // size
    most = 4 * piece_blocks
    pattern = jnp.take(block_pattern, tree_order, axis=0) > 0
    pattern = jnp.concatenate([pattern[:2], pattern[2:] & pattern[:2]], axis=0)
    pattern = pattern.astype(jnp.int32)
    pieces = pattern.reshape(4, col_count, row_count, piece_blocks).transpose(1, 2, 0, 3)
    flat = pieces.reshape(col_count, row_count, most)
    position = (jnp.cumsum(flat, axis=2) - flat).reshape(pieces.shape)
    counts = jnp.sum(flat, axis=2)
    largest = jnp.max(counts)
    own_flat = flat[grid_col, grid_row]
    own_list = jnp.argsort(1 - own_flat, stable=True).astype(jnp.int32)
    supernode = jnp.take(tree_order, own_list // piece_blocks)
    block = own_list % piece_blocks
    half_live = lax.dynamic_slice_in_dim(pattern, grid_col * half_blocks, half_blocks, 1)
    live_rows = lax.dynamic_slice_in_dim(pattern, grid_row * tile_blocks, tile_blocks, 1)
    half_position = position[grid_col].transpose(1, 0, 2).reshape(4, half_blocks)
    k_source = jnp.arange(half_blocks, dtype=jnp.int32) // piece_blocks
    k_order = jnp.argsort(1 - half_live, axis=1, stable=True).astype(jnp.int32)
    k_live = jnp.sum(half_live, axis=1)
    k_count = (k_live + GROUP - 1) // GROUP
    padded = -(-half_blocks // GROUP) * GROUP
    k_order = jnp.pad(k_order, ((0, 0), (0, padded - half_blocks)))
    inside = jnp.arange(padded, dtype=jnp.int32)[None, :] < k_live[:, None]
    k_list = jnp.where(inside, k_order, k_order[:, :1])
    k_any = jnp.max(half_live, axis=0)
    tile_at = grid_row * tile_blocks + jnp.arange(tile_blocks, dtype=jnp.int32)
    own = (tile_at // half_blocks == grid_col).astype(jnp.int32)
    local = tile_at % half_blocks
    window_source = jnp.stack(
        [
            jnp.broadcast_to((local // piece_blocks)[None, :], (4, tile_blocks)),
            jnp.take(half_position, local, axis=1),
        ]
    ).astype(jnp.int32)

    sizes = sorted({max(1, -(-most * part // 12)) for part in (6, 7, 8, 9, 10, 12)})

    def branch(at):
        count = sizes[at]

        def run(_):
            packed = pack(factor_panels, supernode, block, count, size)
            gathered = gather_rows(packed, at)
            place = jnp.take_along_axis(k_source[None, :] * count + half_position, k_list, axis=1)
            place = jnp.where(inside, place, row_count * count).astype(jnp.int32)
            mine = products_of(
                ancestor_inverse, gathered, counts[grid_col], k_list, place, k_count,
                live_rows, k_any, size,
            )
            other = swapped(mine, "col", 0)
            return finish(
                mine, other, coupling, gathered, live_rows, own, tree_order,
                jnp.minimum(window_source, jnp.array([row_count, count])[:, None, None] - 1), size,
            )

        return run

    choice = jnp.sum((largest > jnp.array(sizes[:-1])).astype(jnp.int32))
    inverse_panels, sums = lax.switch(choice, [branch(at) for at in range(len(sizes))], 0)
    totals = lax.psum(sums, ("row", "col"))
    diag_blocks = jnp.take(diag_inverse, tree_order, axis=0)
    parent_diag = [diag_blocks[tree] - totals[tree] for tree in range(2)]
    crosses = [
        -(totals[2 + tree] + multiply(parent_diag[tree], coupling[tree])) for tree in range(2)
    ]
    child_diag = [
        diag_blocks[tree + 2] - totals[4 + tree] - multiply(flipped(coupling[tree]), crosses[tree])
        for tree in range(2)
    ]
    all_diag = jnp.stack(parent_diag + child_diag)
    inverse_diagonal = jnp.take(all_diag, jnp.argsort(tree_order), axis=0)
    return (inverse_panels, inverse_diagonal, jnp.stack(crosses))


def per_device(ancestor_inverse, factor_panels, diag_inverse, coupling, block_pattern, tree_order):
    size = factor_panels.shape[3]
    whole_blocks = math.gcd(ancestor_inverse.shape[1], factor_panels.shape[2]) % size == 0
    run = per_device_blocks if whole_blocks and size % 128 == 0 else per_device_dense
    return run(ancestor_inverse, factor_panels, diag_inverse, coupling, block_pattern, tree_order)


def solution(mesh):
    return jax.shard_map(
        per_device,
        mesh=mesh,
        in_specs=(
            P(None, ("pole", "row"), "col"),
            P(None, None, ("pole", "col", "row"), None),
            P("pole", None, None, None),
            P("pole", None, None, None),
            P(),
            P(),
        ),
        out_specs=(
            P(None, None, ("pole", "row"), None),
            P("pole", None, None, None),
            P("pole", None, None, None),
        ),
        check_vma=False,
    )
```

```python
import functools
import math

import jax
import jax.numpy as jnp
from jax import lax
from jax.experimental import pallas as pl
from jax.experimental.pallas import tpu as pltpu
from jax.sharding import PartitionSpec as P

BF16 = jnp.bfloat16
F32 = jnp.float32
GROUP = 4
VMEM_BYTES = 64 * 1024 * 1024 - 256 * 1024


def swapped(block, axis, bit):
    count = lax.axis_size(axis)
    route = []
    for low in range(count):
        high = low | 1 << bit
        if high != low and high < count:
            route += [(low, high), (high, low)]
    return lax.ppermute(block, axis, route)


def matmul(left_side, right_side):
    return jnp.dot(
        left_side, right_side, preferred_element_type=jnp.float32, precision=lax.Precision.HIGHEST
    )


def multiply(left_side, right_side):
    real_part = matmul(left_side[0], right_side[0]) - matmul(left_side[1], right_side[1])
    imag_part = matmul(left_side[0], right_side[1]) + matmul(left_side[1], right_side[0])
    return jnp.stack([real_part, imag_part])


def flipped(matrix):
    return jnp.swapaxes(matrix, 1, 2)


def row_masks(pattern_eff, first_row, row_count, block_rows):
    row_index = first_row + jnp.arange(row_count, dtype=jnp.int32)
    blocks = row_index // block_rows
    onehot = (blocks[:, None] == jnp.arange(pattern_eff.shape[1], dtype=jnp.int32)[None, :]).astype(
        jnp.float32
    )
    return matmul(pattern_eff, onehot.T)


def per_device_dense(ancestor_inverse, factor_panels, diag_inverse, coupling, block_pattern, tree_order):
    grid_row = lax.axis_index("row")
    grid_col = lax.axis_index("col")
    tile_rows = ancestor_inverse.shape[1]
    half_rows = ancestor_inverse.shape[2]
    piece_rows = factor_panels.shape[2]
    block_rows = factor_panels.shape[3]
    super_count = factor_panels.shape[0]
    share_rows = tile_rows // 2
    sorted_pattern = jnp.take(block_pattern, tree_order, axis=0).astype(jnp.float32)
    pattern_eff = jnp.concatenate(
        [sorted_pattern[:2], sorted_pattern[2:] * sorted_pattern[:2]], axis=0
    )
    source_mask = row_masks(
        pattern_eff, grid_col * half_rows + grid_row * piece_rows, piece_rows, block_rows
    )
    target_mask = row_masks(pattern_eff, grid_row * tile_rows, tile_rows, block_rows)
    panels = jnp.take(factor_panels, tree_order, axis=0) * source_mask[:, None, :, None]
    diag_blocks = jnp.take(diag_inverse, tree_order, axis=0)
    columns = []
    products = []
    for tree_slot in range(super_count):
        gathered = lax.all_gather(panels[tree_slot], "row", axis=1, tiled=True)
        columns.append(gathered)
        products.append(lax.psum(multiply(ancestor_inverse, gathered), "col"))
    own_flag = (grid_row * tile_rows // half_rows == grid_col).astype(jnp.float32)
    offset = jnp.clip(grid_row * tile_rows - grid_col * half_rows, 0, half_rows - tile_rows)
    own_windows = jnp.stack(
        [
            lax.dynamic_slice_in_dim(column_set, offset, tile_rows, 1) * own_flag
            for column_set in columns
        ]
    )
    partner_windows = swapped(own_windows, "col", 0)
    tile_windows = own_windows + partner_windows

    def share(matrix):
        return lax.dynamic_slice_in_dim(matrix, grid_col * share_rows, share_rows, 1)

    windows = [share(tile_windows[tree_slot]) for tree_slot in range(super_count)]
    parent_cols = [
        -target_mask[tree_slot][None, :, None] * products[tree_slot] for tree_slot in range(2)
    ]
    child_cols = [
        -target_mask[tree_slot + 2][None, :, None]
        * (products[tree_slot + 2] + multiply(parent_cols[tree_slot], coupling[tree_slot]))
        for tree_slot in range(2)
    ]
    parent_local = [
        multiply(flipped(windows[tree_slot]), share(parent_cols[tree_slot]))
        for tree_slot in range(2)
    ]
    cross_local = [
        multiply(flipped(share(parent_cols[tree_slot])), windows[tree_slot + 2])
        for tree_slot in range(2)
    ]
    child_local = [
        multiply(flipped(windows[tree_slot + 2]), share(child_cols[tree_slot]))
        for tree_slot in range(2)
    ]
    parent_sums = lax.psum(jnp.stack(parent_local), ("row", "col"))
    parent_diag = [diag_blocks[tree_slot] - parent_sums[tree_slot] for tree_slot in range(2)]
    child_totals = lax.psum(jnp.stack(cross_local + child_local), ("row", "col"))
    crosses = [
        -(child_totals[tree_slot] + multiply(parent_diag[tree_slot], coupling[tree_slot]))
        for tree_slot in range(2)
    ]
    child_sums = [child_totals[2 + tree_slot] for tree_slot in range(2)]
    child_diag = [
        diag_blocks[tree_slot + 2]
        - child_sums[tree_slot]
        - multiply(flipped(coupling[tree_slot]), crosses[tree_slot])
        for tree_slot in range(2)
    ]
    all_cols = jnp.stack(parent_cols + child_cols)
    all_diag = jnp.stack(parent_diag + child_diag)
    inverse_panels = jnp.zeros_like(all_cols).at[tree_order].set(all_cols)
    inverse_diagonal = jnp.zeros_like(all_diag).at[tree_order].set(all_diag)
    return (inverse_panels, inverse_diagonal, jnp.stack(crosses))


def halves(value):
    high = value.astype(BF16)
    return high, (value - high.astype(F32)).astype(BF16)


def pack_kernel(source_ref, panel_ref, packed_ref):
    packed_ref[0] = panel_ref[0].reshape(packed_ref.shape[1:])


def pack(factor_panels, supernode, block, count, size):
    source = jnp.stack([supernode[:count], block[:count]])
    return pl.pallas_call(
        pack_kernel,
        out_shape=jax.ShapeDtypeStruct((count, 2 * size, size), F32),
        grid_spec=pltpu.PrefetchScalarGridSpec(
            num_scalar_prefetch=1,
            grid=(count,),
            in_specs=[
                pl.BlockSpec((1, 2, size, size), lambda g, source: (source[0, g], 0, source[1, g], 0))
            ],
            out_specs=pl.BlockSpec((1, 2 * size, size), lambda g, source: (g, 0, 0)),
        ),
    )(source, factor_panels)


def product_kernel(
    sources, per_source, size, steps_k,
    counts_ref, k_list_ref, place_ref, k_count_ref, row_live_ref, k_any_ref,
    panel_ref, a_ref, out_ref,
    b_high, b_low, a_high, a_low, acc,
):
    step = pl.program_id(0)

    @pl.when(step == 0)
    def _():
        b_high[sources * per_source] = jnp.zeros(b_high.shape[1:], BF16)
        b_low[sources * per_source] = jnp.zeros(b_low.shape[1:], BF16)

    @pl.when(step < sources)
    def _():
        @pl.loop(0, counts_ref[step])
        def _(at):
            block = panel_ref[0, at]
            high, low = halves(jnp.concatenate([block[:size], block[size:]], axis=1))
            b_high[step * per_source + at] = high
            b_low[step * per_source + at] = low

    @pl.when(step >= sources)
    def _():
        row = step - sources
        live = [row_live_ref[slot, row] for slot in range(4)]

        @pl.when(live[0] + live[1] + live[2] + live[3] > 0)
        def _():
            @pl.loop(0, steps_k)
            def _(k):
                @pl.when(k_any_ref[k] > 0)
                def _():
                    columns = pl.ds(pl.multiple_of(k * size, size), size)
                    for part in range(2):
                        high, low = halves(a_ref[part, :, columns])
                        a_high[k, part * size:(part + 1) * size] = high
                        a_low[k, part * size:(part + 1) * size] = low

        for slot in range(4):
            @pl.when(live[slot] == 0)
            def _():
                out_ref[slot] = jnp.zeros(out_ref.shape[1:], F32)

            @pl.when(live[slot] > 0)
            def _():
                acc[...] = jnp.zeros_like(acc)

                @pl.loop(0, k_count_ref[slot])
                def _(group):
                    left, right = [], []
                    for member in range(GROUP):
                        k = k_list_ref[slot, group * GROUP + member]
                        place = place_ref[slot, group * GROUP + member]
                        left += [a_high[k], a_low[k], a_high[k]]
                        right += [b_high[place], b_high[place], b_low[place]]
                    acc[...] += jnp.dot(
                        jnp.concatenate(left, axis=1),
                        jnp.concatenate(right, axis=0),
                        preferred_element_type=F32,
                    )

                out_ref[slot, 0] = acc[:size, :size] - acc[size:, size:]
                out_ref[slot, 1] = acc[:size, size:] + acc[size:, :size]


def products_of(ancestor_inverse, gathered, counts, k_list, place, k_count, row_live, k_any, size):
    sources, per_source = gathered.shape[:2]
    tile_rows, half_rows = ancestor_inverse.shape[1:]
    steps_k = half_rows // size
    rows = tile_rows // size
    return pl.pallas_call(
        functools.partial(product_kernel, sources, per_source, size, steps_k),
        out_shape=jax.ShapeDtypeStruct((4, 2, tile_rows, size), F32),
        grid_spec=pltpu.PrefetchScalarGridSpec(
            num_scalar_prefetch=6,
            grid=(sources + rows,),
            in_specs=[
                pl.BlockSpec(
                    (1, per_source, 2 * size, size),
                    lambda g, *_: (jnp.minimum(g, sources - 1), 0, 0, 0),
                ),
                pl.BlockSpec(
                    (2, size, half_rows), lambda g, *_: (0, jnp.maximum(g - sources, 0), 0)
                ),
            ],
            out_specs=pl.BlockSpec(
                (4, 2, size, size), lambda g, *_: (0, 0, jnp.maximum(g - sources, 0), 0)
            ),
            scratch_shapes=[
                pltpu.VMEM((sources * per_source + 1, size, 2 * size), BF16),
                pltpu.VMEM((sources * per_source + 1, size, 2 * size), BF16),
                pltpu.VMEM((steps_k, 2 * size, size), BF16),
                pltpu.VMEM((steps_k, 2 * size, size), BF16),
                pltpu.VMEM((2 * size, 2 * size), F32),
            ],
        ),
        compiler_params=pltpu.CompilerParams(vmem_limit_bytes=VMEM_BYTES),
    )(counts, k_list, place, k_count, row_live, k_any, gathered, ancestor_inverse)


def wide(matrix):
    return jnp.concatenate([matrix[0], matrix[1]], axis=1)


def folded(product, size, transposed):
    return jnp.stack(
        [
            product[:size, :size] - product[size:, size:],
            product[:size, size:] + product[size:, :size],
        ]
    )


def contracted(left_side, right_side):
    return lax.dot_general(
        left_side, right_side, (((0,), (0,)), ((), ())),
        preferred_element_type=F32, precision=lax.Precision.HIGHEST,
    )


def finish_kernel(
    size, live_ref, own_ref, order_ref, source_ref,
    mine_ref, other_ref, link_ref, w0_ref, w1_ref, w2_ref, w3_ref,
    columns_ref, sums_ref,
):
    row = pl.program_id(0)
    windows = (w0_ref, w1_ref, w2_ref, w3_ref)

    @pl.when(row == 0)
    def _():
        sums_ref[...] = jnp.zeros_like(sums_ref)

    def window(slot):
        block = windows[slot][0, 0]
        return jnp.concatenate([block[:size], block[size:]], axis=1)

    for tree in range(2):
        child = tree + 2
        parent_at = order_ref[tree]
        child_at = order_ref[child]

        @pl.when(live_ref[tree, row] == 0)
        def _():
            columns_ref[parent_at] = jnp.zeros(columns_ref.shape[1:], F32)

        @pl.when(live_ref[child, row] == 0)
        def _():
            columns_ref[child_at] = jnp.zeros(columns_ref.shape[1:], F32)

        @pl.when(live_ref[tree, row] > 0)
        def _():
            columns_ref[parent_at] = -(mine_ref[tree] + other_ref[tree])

            @pl.when(own_ref[row] > 0)
            def _():
                sums_ref[tree] += folded(
                    contracted(window(tree), wide(columns_ref[parent_at])), size, True
                )

        @pl.when(live_ref[child, row] > 0)
        def _():
            parent = columns_ref[parent_at]
            linked = folded(
                matmul(jnp.concatenate([parent[0], parent[1]], axis=0), wide(link_ref[tree])),
                size, False,
            )
            columns_ref[child_at] = -(mine_ref[child] + other_ref[child] + linked)

            @pl.when(own_ref[row] > 0)
            def _():
                other_window = window(child)
                sums_ref[child] += folded(
                    contracted(wide(parent), other_window), size, True
                )
                sums_ref[tree + 4] += folded(
                    contracted(other_window, wide(columns_ref[child_at])), size, True
                )


def finish(mine, other, coupling, gathered, live, own, tree_order, source, size):
    rows = live.shape[1]

    def window_map(slot, g, live, own, order, source):
        return (source[0, slot, g], source[1, slot, g], 0, 0)

    return pl.pallas_call(
        functools.partial(finish_kernel, size),
        out_shape=(
            jax.ShapeDtypeStruct(mine.shape, F32),
            jax.ShapeDtypeStruct((6, 2, size, size), F32),
        ),
        grid_spec=pltpu.PrefetchScalarGridSpec(
            num_scalar_prefetch=4,
            grid=(rows,),
            in_specs=[
                pl.BlockSpec((4, 2, size, size), lambda g, *_: (0, 0, g, 0)),
                pl.BlockSpec((4, 2, size, size), lambda g, *_: (0, 0, g, 0)),
                pl.BlockSpec(coupling.shape, lambda g, *_: (0, 0, 0, 0)),
            ]
            + [
                pl.BlockSpec((1, 1, 2 * size, size), functools.partial(window_map, slot))
                for slot in range(4)
            ],
            out_specs=(
                pl.BlockSpec((4, 2, size, size), lambda g, *_: (0, 0, g, 0)),
                pl.BlockSpec((6, 2, size, size), lambda g, *_: (0, 0, 0, 0)),
            ),
        ),
        compiler_params=pltpu.CompilerParams(vmem_limit_bytes=VMEM_BYTES),
    )(live, own, tree_order, source, mine, other, coupling, gathered, gathered, gathered, gathered)


def relay_kernel(rows, first, own_ref, all_ref, staged, send_sem, recv_sem, load_sem, keep_sem):
    here = lax.axis_index("row")
    lines = rows // 2
    z, y = here // 2, here % 2
    count = own_ref.shape[0]
    parts = (pl.ds(0, first), pl.ds(first, count - first))
    beside = z * 2 + (1 - y)
    up, down = here + 2, here - 2
    has_up, has_down = z < lines - 1, z > 0

    def copy(path, origin, way, target, own=False):
        part = parts[path]
        return pltpu.make_async_remote_copy(
            src_ref=own_ref.at[part] if own else all_ref.at[origin, part],
            dst_ref=all_ref.at[origin, part],
            send_sem=send_sem.at[path, origin, way],
            recv_sem=recv_sem.at[path, origin],
            device_id={"row": target},
            device_id_type=pl.DeviceIdType.MESH,
        )

    def arrived(path, origin):
        copy(path, origin, 0, beside).wait_recv()

    barrier = pltpu.get_barrier_semaphore()

    def greet(target):
        pl.semaphore_signal(
            barrier, inc=1, device_id={"row": target}, device_id_type=pl.DeviceIdType.MESH
        )

    greet(beside)

    @pl.when(has_up)
    def _():
        greet(up)

    @pl.when(has_down)
    def _():
        greet(down)

    pl.semaphore_wait(barrier, 1 + has_up.astype(jnp.int32) + has_down.astype(jnp.int32))

    copy(0, here, 2, beside, True).start()
    for path in (1, 0):
        @pl.when(has_up)
        def _():
            copy(path, here, 0, up, True).start()

        @pl.when(has_down)
        def _():
            copy(path, here, 1, down, True).start()

    copy(1, here, 2, beside, True).start()
    load = pltpu.make_async_copy(own_ref, staged, load_sem)
    load.start()
    load.wait()
    keep = pltpu.make_async_copy(staged, all_ref.at[here], keep_sem)
    keep.start()
    arrived(0, beside)

    @pl.when(has_up)
    def _():
        copy(0, beside, 0, up).start()

    @pl.when(has_down)
    def _():
        copy(0, beside, 1, down).start()

    for distance in range(1, lines):
        for path, sides in ((1, (here,)), (0, (here, beside))):
            for side in sides:
                below, above = side - 2 * distance, side + 2 * distance

                @pl.when(z - distance >= 0)
                def _():
                    arrived(path, below)

                    @pl.when(has_up)
                    def _():
                        copy(path, below, 0, up).start()

                    if path == 1:
                        copy(path, below, 2, beside).start()

                @pl.when(z + distance < lines)
                def _():
                    arrived(path, above)

                    @pl.when(has_down)
                    def _():
                        copy(path, above, 1, down).start()

                    if path == 1:
                        copy(path, above, 2, beside).start()

    for line in range(lines):
        arrived(1, line * 2 + (1 - y))
    keep.wait()

    copy(0, here, 2, beside, True).wait_send()
    for line in range(lines):
        copy(1, line * 2 + y, 2, beside).wait_send()
        for path, origin in ((1, line * 2 + y), (0, line * 2 + y), (0, line * 2 + 1 - y)):
            @pl.when(has_up & (line <= z))
            def _():
                copy(path, origin, 0, up).wait_send()

            @pl.when(has_down & (line >= z))
            def _():
                copy(path, origin, 1, down).wait_send()


def gather_rows(packed, branch):
    rows = lax.axis_size("row")
    count = packed.shape[0]
    if rows % 2 or rows < 4 or count < 2:
        return lax.all_gather(packed, "row", axis=0, tiled=False)
    first = max(1, round(count / 6))
    return pl.pallas_call(
        functools.partial(relay_kernel, rows, first),
        out_shape=jax.ShapeDtypeStruct((rows,) + packed.shape, F32),
        in_specs=[pl.BlockSpec(memory_space=pl.ANY)],
        out_specs=pl.BlockSpec(memory_space=pl.ANY),
        scratch_shapes=[
            pltpu.VMEM(packed.shape, F32),
            pltpu.SemaphoreType.DMA((2, rows, 3)),
            pltpu.SemaphoreType.DMA((2, rows)),
            pltpu.SemaphoreType.DMA,
            pltpu.SemaphoreType.DMA,
        ],
        compiler_params=pltpu.CompilerParams(collective_id=branch + 1, has_side_effects=True),
    )(packed)


def sum_kernel(stages, part_ref, sum_ref, total, landed, send_sem, recv_sem):
    barrier = pltpu.get_barrier_semaphore()
    partners = []
    for axis, bit in stages:
        at = lax.axis_index(axis)
        mine = (at // (1 << bit)) % 2
        partners.append((axis, at + (1 << bit) * (1 - 2 * mine), mine))
    for axis, partner, _ in partners:
        pl.semaphore_signal(
            barrier, inc=1, device_id={axis: partner}, device_id_type=pl.DeviceIdType.MESH
        )
    pl.semaphore_wait(barrier, len(stages))

    total[...] = part_ref[...]
    length = part_ref.shape[0]
    start, landing = 0, 0
    spans = []
    for stage, (axis, partner, mine) in enumerate(partners):
        length = length // 2
        keep = pl.multiple_of(start + mine * length, 8)
        give = pl.multiple_of(start + (1 - mine) * length, 8)
        copy = pltpu.make_async_remote_copy(
            src_ref=total.at[pl.ds(give, length)],
            dst_ref=landed.at[pl.ds(landing, length)],
            send_sem=send_sem.at[stage],
            recv_sem=recv_sem.at[stage],
            device_id={axis: partner},
            device_id_type=pl.DeviceIdType.MESH,
        )
        copy.start()
        copy.wait()
        total[pl.ds(keep, length)] += landed[pl.ds(landing, length)]
        spans.append((keep, length))
        start, landing = keep, landing + length
    sum_ref[pl.ds(start, length)] = total[pl.ds(start, length)]
    for stage in reversed(range(len(stages))):
        axis, partner, _ = partners[stage]
        keep, length = spans[stage]
        copy = pltpu.make_async_remote_copy(
            src_ref=sum_ref.at[pl.ds(keep, length)],
            dst_ref=sum_ref.at[pl.ds(keep, length)],
            send_sem=send_sem.at[len(stages) + stage],
            recv_sem=recv_sem.at[len(stages) + stage],
            device_id={axis: partner},
            device_id_type=pl.DeviceIdType.MESH,
        )
        copy.start()
        copy.wait()


def summed(parts):
    stages = []
    for axis in ("col", "row"):
        count = lax.axis_size(axis)
        if count & (count - 1):
            return lax.psum(parts, ("row", "col"))
        stages += [(axis, bit) for bit in range(count.bit_length() - 1)]
    flat = parts.reshape(-1, parts.shape[-1])
    if flat.shape[0] % (8 << len(stages)) or not stages:
        return lax.psum(parts, ("row", "col"))
    total = pl.pallas_call(
        functools.partial(sum_kernel, stages),
        out_shape=jax.ShapeDtypeStruct(flat.shape, F32),
        in_specs=[pl.BlockSpec(memory_space=pltpu.VMEM)],
        out_specs=pl.BlockSpec(memory_space=pltpu.VMEM),
        scratch_shapes=[
            pltpu.VMEM(flat.shape, F32),
            pltpu.VMEM(flat.shape, F32),
            pltpu.SemaphoreType.DMA((2 * len(stages),)),
            pltpu.SemaphoreType.DMA((2 * len(stages),)),
        ],
        compiler_params=pltpu.CompilerParams(collective_id=0, has_side_effects=True),
    )(flat)
    return total.reshape(parts.shape)


def per_device_blocks(
    ancestor_inverse, factor_panels, diag_inverse, coupling, block_pattern, tree_order
):
    grid_row = lax.axis_index("row")
    grid_col = lax.axis_index("col")
    row_count = lax.axis_size("row")
    col_count = lax.axis_size("col")
    size = factor_panels.shape[3]
    tile_blocks = ancestor_inverse.shape[1] // size
    half_blocks = ancestor_inverse.shape[2] // size
    piece_blocks = factor_panels.shape[2] // size
    most = 4 * piece_blocks
    pattern = jnp.take(block_pattern, tree_order, axis=0) > 0
    pattern = jnp.concatenate([pattern[:2], pattern[2:] & pattern[:2]], axis=0)
    pattern = pattern.astype(jnp.int32)
    pieces = pattern.reshape(4, col_count, row_count, piece_blocks).transpose(1, 2, 0, 3)
    flat = pieces.reshape(col_count, row_count, most)
    position = (jnp.cumsum(flat, axis=2) - flat).reshape(pieces.shape)
    counts = jnp.sum(flat, axis=2)
    largest = jnp.max(counts)
    own_flat = flat[grid_col, grid_row]
    own_list = jnp.argsort(1 - own_flat, stable=True).astype(jnp.int32)
    supernode = jnp.take(tree_order, own_list // piece_blocks)
    block = own_list % piece_blocks
    half_live = lax.dynamic_slice_in_dim(pattern, grid_col * half_blocks, half_blocks, 1)
    live_rows = lax.dynamic_slice_in_dim(pattern, grid_row * tile_blocks, tile_blocks, 1)
    half_position = position[grid_col].transpose(1, 0, 2).reshape(4, half_blocks)
    k_source = jnp.arange(half_blocks, dtype=jnp.int32) // piece_blocks
    k_order = jnp.argsort(1 - half_live, axis=1, stable=True).astype(jnp.int32)
    k_live = jnp.sum(half_live, axis=1)
    k_count = (k_live + GROUP - 1) // GROUP
    padded = -(-half_blocks // GROUP) * GROUP
    k_order = jnp.pad(k_order, ((0, 0), (0, padded - half_blocks)))
    inside = jnp.arange(padded, dtype=jnp.int32)[None, :] < k_live[:, None]
    k_list = jnp.where(inside, k_order, k_order[:, :1])
    k_any = jnp.max(half_live, axis=0)
    tile_at = grid_row * tile_blocks + jnp.arange(tile_blocks, dtype=jnp.int32)
    own = (tile_at // half_blocks == grid_col).astype(jnp.int32)
    local = tile_at % half_blocks
    window_source = jnp.stack(
        [
            jnp.broadcast_to((local // piece_blocks)[None, :], (4, tile_blocks)),
            jnp.take(half_position, local, axis=1),
        ]
    ).astype(jnp.int32)

    sizes = sorted({max(1, -(-most * part // 12)) for part in (7, 8, 9, 10, 12)})

    def branch(at):
        count = sizes[at]

        def run(_):
            packed = pack(factor_panels, supernode, block, count, size)
            gathered = gather_rows(packed, at)
            place = jnp.take_along_axis(k_source[None, :] * count + half_position, k_list, axis=1)
            place = jnp.where(inside, place, row_count * count).astype(jnp.int32)
            mine = products_of(
                ancestor_inverse, gathered, counts[grid_col], k_list, place, k_count,
                live_rows, k_any, size,
            )
            other = swapped(mine, "col", 0)
            return finish(
                mine, other, coupling, gathered, live_rows, own, tree_order,
                jnp.minimum(window_source, jnp.array([row_count, count])[:, None, None] - 1), size,
            )

        return run

    choice = jnp.sum((largest > jnp.array(sizes[:-1])).astype(jnp.int32))
    inverse_panels, sums = lax.switch(choice, [branch(at) for at in range(len(sizes))], 0)
    totals = summed(sums)
    diag_blocks = jnp.take(diag_inverse, tree_order, axis=0)
    parent_diag = [diag_blocks[tree] - totals[tree] for tree in range(2)]
    crosses = [
        -(totals[2 + tree] + multiply(parent_diag[tree], coupling[tree])) for tree in range(2)
    ]
    child_diag = [
        diag_blocks[tree + 2] - totals[4 + tree] - multiply(flipped(coupling[tree]), crosses[tree])
        for tree in range(2)
    ]
    all_diag = jnp.stack(parent_diag + child_diag)
    inverse_diagonal = jnp.take(all_diag, jnp.argsort(tree_order), axis=0)
    return (inverse_panels, inverse_diagonal, jnp.stack(crosses))


def per_device(ancestor_inverse, factor_panels, diag_inverse, coupling, block_pattern, tree_order):
    size = factor_panels.shape[3]
    whole_blocks = math.gcd(ancestor_inverse.shape[1], factor_panels.shape[2]) % size == 0
    run = per_device_blocks if whole_blocks and size % 128 == 0 else per_device_dense
    return run(ancestor_inverse, factor_panels, diag_inverse, coupling, block_pattern, tree_order)


def solution(mesh):
    return jax.shard_map(
        per_device,
        mesh=mesh,
        in_specs=(
            P(None, ("pole", "row"), "col"),
            P(None, None, ("pole", "col", "row"), None),
            P("pole", None, None, None),
            P("pole", None, None, None),
            P(),
            P(),
        ),
        out_specs=(
            P(None, None, ("pole", "row"), None),
            P("pole", None, None, None),
            P("pole", None, None, None),
        ),
        check_vma=False,
    )
```

```python
import functools
import math

import jax
import jax.numpy as jnp
from jax import lax
from jax.experimental import pallas as pl
from jax.experimental.pallas import tpu as pltpu
from jax.sharding import PartitionSpec as P

BF16 = jnp.bfloat16
F32 = jnp.float32
GROUP = 8
VMEM_BYTES = 64 * 1024 * 1024 - 256 * 1024


def swapped(block, axis, bit):
    count = lax.axis_size(axis)
    route = []
    for low in range(count):
        high = low | 1 << bit
        if high != low and high < count:
            route += [(low, high), (high, low)]
    return lax.ppermute(block, axis, route)


def matmul(left_side, right_side):
    return jnp.dot(
        left_side, right_side, preferred_element_type=jnp.float32, precision=lax.Precision.HIGHEST
    )


def multiply(left_side, right_side):
    real_part = matmul(left_side[0], right_side[0]) - matmul(left_side[1], right_side[1])
    imag_part = matmul(left_side[0], right_side[1]) + matmul(left_side[1], right_side[0])
    return jnp.stack([real_part, imag_part])


def flipped(matrix):
    return jnp.swapaxes(matrix, 1, 2)


def row_masks(pattern_eff, first_row, row_count, block_rows):
    row_index = first_row + jnp.arange(row_count, dtype=jnp.int32)
    blocks = row_index // block_rows
    onehot = (blocks[:, None] == jnp.arange(pattern_eff.shape[1], dtype=jnp.int32)[None, :]).astype(
        jnp.float32
    )
    return matmul(pattern_eff, onehot.T)


def per_device_dense(ancestor_inverse, factor_panels, diag_inverse, coupling, block_pattern, tree_order):
    grid_row = lax.axis_index("row")
    grid_col = lax.axis_index("col")
    tile_rows = ancestor_inverse.shape[1]
    half_rows = ancestor_inverse.shape[2]
    piece_rows = factor_panels.shape[2]
    block_rows = factor_panels.shape[3]
    super_count = factor_panels.shape[0]
    share_rows = tile_rows // 2
    sorted_pattern = jnp.take(block_pattern, tree_order, axis=0).astype(jnp.float32)
    pattern_eff = jnp.concatenate(
        [sorted_pattern[:2], sorted_pattern[2:] * sorted_pattern[:2]], axis=0
    )
    source_mask = row_masks(
        pattern_eff, grid_col * half_rows + grid_row * piece_rows, piece_rows, block_rows
    )
    target_mask = row_masks(pattern_eff, grid_row * tile_rows, tile_rows, block_rows)
    panels = jnp.take(factor_panels, tree_order, axis=0) * source_mask[:, None, :, None]
    diag_blocks = jnp.take(diag_inverse, tree_order, axis=0)
    columns = []
    products = []
    for tree_slot in range(super_count):
        gathered = lax.all_gather(panels[tree_slot], "row", axis=1, tiled=True)
        columns.append(gathered)
        products.append(lax.psum(multiply(ancestor_inverse, gathered), "col"))
    own_flag = (grid_row * tile_rows // half_rows == grid_col).astype(jnp.float32)
    offset = jnp.clip(grid_row * tile_rows - grid_col * half_rows, 0, half_rows - tile_rows)
    own_windows = jnp.stack(
        [
            lax.dynamic_slice_in_dim(column_set, offset, tile_rows, 1) * own_flag
            for column_set in columns
        ]
    )
    partner_windows = swapped(own_windows, "col", 0)
    tile_windows = own_windows + partner_windows

    def share(matrix):
        return lax.dynamic_slice_in_dim(matrix, grid_col * share_rows, share_rows, 1)

    windows = [share(tile_windows[tree_slot]) for tree_slot in range(super_count)]
    parent_cols = [
        -target_mask[tree_slot][None, :, None] * products[tree_slot] for tree_slot in range(2)
    ]
    child_cols = [
        -target_mask[tree_slot + 2][None, :, None]
        * (products[tree_slot + 2] + multiply(parent_cols[tree_slot], coupling[tree_slot]))
        for tree_slot in range(2)
    ]
    parent_local = [
        multiply(flipped(windows[tree_slot]), share(parent_cols[tree_slot]))
        for tree_slot in range(2)
    ]
    cross_local = [
        multiply(flipped(share(parent_cols[tree_slot])), windows[tree_slot + 2])
        for tree_slot in range(2)
    ]
    child_local = [
        multiply(flipped(windows[tree_slot + 2]), share(child_cols[tree_slot]))
        for tree_slot in range(2)
    ]
    parent_sums = lax.psum(jnp.stack(parent_local), ("row", "col"))
    parent_diag = [diag_blocks[tree_slot] - parent_sums[tree_slot] for tree_slot in range(2)]
    child_totals = lax.psum(jnp.stack(cross_local + child_local), ("row", "col"))
    crosses = [
        -(child_totals[tree_slot] + multiply(parent_diag[tree_slot], coupling[tree_slot]))
        for tree_slot in range(2)
    ]
    child_sums = [child_totals[2 + tree_slot] for tree_slot in range(2)]
    child_diag = [
        diag_blocks[tree_slot + 2]
        - child_sums[tree_slot]
        - multiply(flipped(coupling[tree_slot]), crosses[tree_slot])
        for tree_slot in range(2)
    ]
    all_cols = jnp.stack(parent_cols + child_cols)
    all_diag = jnp.stack(parent_diag + child_diag)
    inverse_panels = jnp.zeros_like(all_cols).at[tree_order].set(all_cols)
    inverse_diagonal = jnp.zeros_like(all_diag).at[tree_order].set(all_diag)
    return (inverse_panels, inverse_diagonal, jnp.stack(crosses))


def halves(value):
    high = value.astype(BF16)
    return high, (value - high.astype(F32)).astype(BF16)


def pack_kernel(source_ref, *refs):
    *panel_refs, packed_ref = refs
    for at, panel_ref in enumerate(panel_refs):
        packed_ref[at] = panel_ref[0].reshape(packed_ref.shape[1:])


def pack(factor_panels, supernode, block, size):
    count = block.shape[0]
    together = math.gcd(count, 4)

    def panel_map(at, g, source):
        return (source[0, g * together + at], 0, source[1, g * together + at], 0)

    return pl.pallas_call(
        pack_kernel,
        out_shape=jax.ShapeDtypeStruct((count, 2 * size, size), F32),
        grid_spec=pltpu.PrefetchScalarGridSpec(
            num_scalar_prefetch=1,
            grid=(count // together,),
            in_specs=[
                pl.BlockSpec((1, 2, size, size), functools.partial(panel_map, at))
                for at in range(together)
            ],
            out_specs=pl.BlockSpec((together, 2 * size, size), lambda g, source: (g, 0, 0)),
        ),
    )(jnp.stack([supernode, block]), *[factor_panels] * together)


def product_kernel(
    sources, per_source, size, steps_k,
    counts_ref, k_list_ref, place_ref, k_count_ref, row_live_ref, k_any_ref,
    panel_ref, a_ref, out_ref,
    b_high, b_low, a_high, a_low, acc,
):
    step = pl.program_id(0)

    @pl.when(step == 0)
    def _():
        b_high[sources * per_source] = jnp.zeros(b_high.shape[1:], BF16)
        b_low[sources * per_source] = jnp.zeros(b_low.shape[1:], BF16)

    @pl.when(step < sources)
    def _():
        @pl.loop(0, counts_ref[step])
        def _(at):
            block = panel_ref[0, at]
            high, low = halves(jnp.concatenate([block[:size], block[size:]], axis=1))
            b_high[step * per_source + at] = high
            b_low[step * per_source + at] = low

    @pl.when(step >= sources)
    def _():
        row = step - sources
        live = [row_live_ref[slot, row] for slot in range(4)]

        @pl.when(live[0] + live[1] + live[2] + live[3] > 0)
        def _():
            @pl.loop(0, steps_k)
            def _(k):
                @pl.when(k_any_ref[k] > 0)
                def _():
                    columns = pl.ds(pl.multiple_of(k * size, size), size)
                    for part in range(2):
                        high, low = halves(a_ref[part, :, columns])
                        a_high[k, part * size:(part + 1) * size] = high
                        a_low[k, part * size:(part + 1) * size] = low

        for slot in range(4):
            @pl.when(live[slot] == 0)
            def _():
                out_ref[slot] = jnp.zeros(out_ref.shape[1:], F32)

            @pl.when(live[slot] > 0)
            def _():
                acc[...] = jnp.zeros_like(acc)

                @pl.loop(0, k_count_ref[slot])
                def _(group):
                    left, right = [], []
                    for member in range(GROUP):
                        k = k_list_ref[slot, group * GROUP + member]
                        place = place_ref[slot, group * GROUP + member]
                        left += [a_high[k], a_low[k], a_high[k]]
                        right += [b_high[place], b_high[place], b_low[place]]
                    acc[...] += jnp.dot(
                        jnp.concatenate(left, axis=1),
                        jnp.concatenate(right, axis=0),
                        preferred_element_type=F32,
                    )

                out_ref[slot, 0] = acc[:size, :size] - acc[size:, size:]
                out_ref[slot, 1] = acc[:size, size:] + acc[size:, :size]


def products_of(ancestor_inverse, gathered, counts, k_list, place, k_count, row_live, k_any, size):
    sources, per_source = gathered.shape[:2]
    tile_rows, half_rows = ancestor_inverse.shape[1:]
    steps_k = half_rows // size
    rows = tile_rows // size
    return pl.pallas_call(
        functools.partial(product_kernel, sources, per_source, size, steps_k),
        out_shape=jax.ShapeDtypeStruct((4, 2, tile_rows, size), F32),
        grid_spec=pltpu.PrefetchScalarGridSpec(
            num_scalar_prefetch=6,
            grid=(sources + rows,),
            in_specs=[
                pl.BlockSpec(
                    (1, per_source, 2 * size, size),
                    lambda g, *_: (jnp.minimum(g, sources - 1), 0, 0, 0),
                ),
                pl.BlockSpec(
                    (2, size, half_rows), lambda g, *_: (0, jnp.maximum(g - sources, 0), 0)
                ),
            ],
            out_specs=pl.BlockSpec(
                (4, 2, size, size), lambda g, *_: (0, 0, jnp.maximum(g - sources, 0), 0)
            ),
            scratch_shapes=[
                pltpu.VMEM((sources * per_source + 1, size, 2 * size), BF16),
                pltpu.VMEM((sources * per_source + 1, size, 2 * size), BF16),
                pltpu.VMEM((steps_k, 2 * size, size), BF16),
                pltpu.VMEM((steps_k, 2 * size, size), BF16),
                pltpu.VMEM((2 * size, 2 * size), F32),
            ],
        ),
        compiler_params=pltpu.CompilerParams(vmem_limit_bytes=VMEM_BYTES),
    )(counts, k_list, place, k_count, row_live, k_any, gathered, ancestor_inverse)


def wide(matrix):
    return jnp.concatenate([matrix[0], matrix[1]], axis=1)


def folded(product, size, transposed):
    return jnp.stack(
        [
            product[:size, :size] - product[size:, size:],
            product[:size, size:] + product[size:, :size],
        ]
    )


def contracted(left_side, right_side):
    return lax.dot_general(
        left_side, right_side, (((0,), (0,)), ((), ())),
        preferred_element_type=F32, precision=lax.Precision.HIGHEST,
    )


def finish_kernel(
    size, live_ref, own_ref, order_ref, source_ref,
    mine_ref, other_ref, link_ref, w0_ref, w1_ref, w2_ref, w3_ref,
    columns_ref, sums_ref,
):
    row = pl.program_id(0)
    windows = (w0_ref, w1_ref, w2_ref, w3_ref)

    @pl.when(row == 0)
    def _():
        sums_ref[...] = jnp.zeros_like(sums_ref)

    def window(slot):
        block = windows[slot][0, 0]
        return jnp.concatenate([block[:size], block[size:]], axis=1)

    for tree in range(2):
        child = tree + 2
        parent_at = order_ref[tree]
        child_at = order_ref[child]

        @pl.when(live_ref[tree, row] == 0)
        def _():
            columns_ref[parent_at] = jnp.zeros(columns_ref.shape[1:], F32)

        @pl.when(live_ref[child, row] == 0)
        def _():
            columns_ref[child_at] = jnp.zeros(columns_ref.shape[1:], F32)

        @pl.when(live_ref[tree, row] > 0)
        def _():
            columns_ref[parent_at] = -(mine_ref[tree] + other_ref[tree])

            @pl.when(own_ref[row] > 0)
            def _():
                sums_ref[tree] += folded(
                    contracted(window(tree), wide(columns_ref[parent_at])), size, True
                )

        @pl.when(live_ref[child, row] > 0)
        def _():
            parent = columns_ref[parent_at]
            linked = folded(
                matmul(jnp.concatenate([parent[0], parent[1]], axis=0), wide(link_ref[tree])),
                size, False,
            )
            columns_ref[child_at] = -(mine_ref[child] + other_ref[child] + linked)

            @pl.when(own_ref[row] > 0)
            def _():
                other_window = window(child)
                sums_ref[child] += folded(
                    contracted(wide(parent), other_window), size, True
                )
                sums_ref[tree + 4] += folded(
                    contracted(other_window, wide(columns_ref[child_at])), size, True
                )


def finish(mine, other, coupling, gathered, live, own, tree_order, source, size):
    rows = live.shape[1]

    def window_map(slot, g, live, own, order, source):
        return (source[0, slot, g], source[1, slot, g], 0, 0)

    return pl.pallas_call(
        functools.partial(finish_kernel, size),
        out_shape=(
            jax.ShapeDtypeStruct(mine.shape, F32),
            jax.ShapeDtypeStruct((6, 2, size, size), F32),
        ),
        grid_spec=pltpu.PrefetchScalarGridSpec(
            num_scalar_prefetch=4,
            grid=(rows,),
            in_specs=[
                pl.BlockSpec((4, 2, size, size), lambda g, *_: (0, 0, g, 0)),
                pl.BlockSpec((4, 2, size, size), lambda g, *_: (0, 0, g, 0)),
                pl.BlockSpec(coupling.shape, lambda g, *_: (0, 0, 0, 0)),
            ]
            + [
                pl.BlockSpec((1, 1, 2 * size, size), functools.partial(window_map, slot))
                for slot in range(4)
            ],
            out_specs=(
                pl.BlockSpec((4, 2, size, size), lambda g, *_: (0, 0, g, 0)),
                pl.BlockSpec((6, 2, size, size), lambda g, *_: (0, 0, 0, 0)),
            ),
        ),
        compiler_params=pltpu.CompilerParams(vmem_limit_bytes=VMEM_BYTES),
    )(live, own, tree_order, source, mine, other, coupling, gathered, gathered, gathered, gathered)


def relay_kernel(rows, count, first, own_ref, all_ref, staged, send_sem, recv_sem, load_sem, keep_sem):
    here = lax.axis_index("row")
    lines = rows // 2
    z, y = here // 2, here % 2
    parts = (pl.ds(0, first), pl.ds(first, count - first))
    beside = z * 2 + (1 - y)
    up, down = here + 2, here - 2
    has_up, has_down = z < lines - 1, z > 0

    def copy(path, origin, way, target, own=False):
        part = parts[path]
        return pltpu.make_async_remote_copy(
            src_ref=own_ref.at[part] if own else all_ref.at[origin, part],
            dst_ref=all_ref.at[origin, part],
            send_sem=send_sem.at[path, origin, way],
            recv_sem=recv_sem.at[path, origin],
            device_id={"row": target},
            device_id_type=pl.DeviceIdType.MESH,
        )

    def arrived(path, origin):
        copy(path, origin, 0, beside).wait_recv()

    barrier = pltpu.get_barrier_semaphore()

    def greet(target):
        pl.semaphore_signal(
            barrier, inc=1, device_id={"row": target}, device_id_type=pl.DeviceIdType.MESH
        )

    greet(beside)

    @pl.when(has_up)
    def _():
        greet(up)

    @pl.when(has_down)
    def _():
        greet(down)

    pl.semaphore_wait(barrier, 1 + has_up.astype(jnp.int32) + has_down.astype(jnp.int32))

    copy(0, here, 2, beside, True).start()
    for path in (1, 0):
        @pl.when(has_up)
        def _():
            copy(path, here, 0, up, True).start()

        @pl.when(has_down)
        def _():
            copy(path, here, 1, down, True).start()

    copy(1, here, 2, beside, True).start()
    load = pltpu.make_async_copy(own_ref.at[pl.ds(0, count)], staged, load_sem)
    load.start()
    load.wait()
    keep = pltpu.make_async_copy(staged, all_ref.at[here, pl.ds(0, count)], keep_sem)
    keep.start()
    arrived(0, beside)

    @pl.when(has_up)
    def _():
        copy(0, beside, 0, up).start()

    @pl.when(has_down)
    def _():
        copy(0, beside, 1, down).start()

    for distance in range(1, lines):
        for path, sides in ((1, (here,)), (0, (here, beside))):
            for side in sides:
                below, above = side - 2 * distance, side + 2 * distance

                @pl.when(z - distance >= 0)
                def _():
                    arrived(path, below)

                    @pl.when(has_up)
                    def _():
                        copy(path, below, 0, up).start()

                    if path == 1:
                        copy(path, below, 2, beside).start()

                @pl.when(z + distance < lines)
                def _():
                    arrived(path, above)

                    @pl.when(has_down)
                    def _():
                        copy(path, above, 1, down).start()

                    if path == 1:
                        copy(path, above, 2, beside).start()

    for line in range(lines):
        arrived(1, line * 2 + (1 - y))
    keep.wait()

    copy(0, here, 2, beside, True).wait_send()
    for line in range(lines):
        copy(1, line * 2 + y, 2, beside).wait_send()
        for path, origin in ((1, line * 2 + y), (0, line * 2 + y), (0, line * 2 + 1 - y)):
            @pl.when(has_up & (line <= z))
            def _():
                copy(path, origin, 0, up).wait_send()

            @pl.when(has_down & (line >= z))
            def _():
                copy(path, origin, 1, down).wait_send()


def gather_rows(packed, count, branch):
    rows = lax.axis_size("row")
    if rows % 2 or rows < 4 or count < 2:
        return lax.all_gather(packed, "row", axis=0, tiled=False)
    first = max(1, round(count / 6))
    return pl.pallas_call(
        functools.partial(relay_kernel, rows, count, first),
        out_shape=jax.ShapeDtypeStruct((rows,) + packed.shape, F32),
        in_specs=[pl.BlockSpec(memory_space=pl.ANY)],
        out_specs=pl.BlockSpec(memory_space=pl.ANY),
        scratch_shapes=[
            pltpu.VMEM((count,) + packed.shape[1:], F32),
            pltpu.SemaphoreType.DMA((2, rows, 3)),
            pltpu.SemaphoreType.DMA((2, rows)),
            pltpu.SemaphoreType.DMA,
            pltpu.SemaphoreType.DMA,
        ],
        compiler_params=pltpu.CompilerParams(collective_id=branch + 1, has_side_effects=True),
    )(packed)


def sum_kernel(stages, part_ref, sum_ref, total, landed, send_sem, recv_sem):
    barrier = pltpu.get_barrier_semaphore()
    partners = []
    for axis, bit in stages:
        at = lax.axis_index(axis)
        mine = (at // (1 << bit)) % 2
        partners.append((axis, at + (1 << bit) * (1 - 2 * mine), mine))
    for axis, partner, _ in partners:
        pl.semaphore_signal(
            barrier, inc=1, device_id={axis: partner}, device_id_type=pl.DeviceIdType.MESH
        )
    pl.semaphore_wait(barrier, len(stages))

    total[...] = part_ref[...]
    length = part_ref.shape[0]
    start, landing = 0, 0
    spans = []
    for stage, (axis, partner, mine) in enumerate(partners):
        length = length // 2
        keep = pl.multiple_of(start + mine * length, 8)
        give = pl.multiple_of(start + (1 - mine) * length, 8)
        copy = pltpu.make_async_remote_copy(
            src_ref=total.at[pl.ds(give, length)],
            dst_ref=landed.at[pl.ds(landing, length)],
            send_sem=send_sem.at[stage],
            recv_sem=recv_sem.at[stage],
            device_id={axis: partner},
            device_id_type=pl.DeviceIdType.MESH,
        )
        copy.start()
        copy.wait()
        total[pl.ds(keep, length)] += landed[pl.ds(landing, length)]
        spans.append((keep, length))
        start, landing = keep, landing + length
    sum_ref[pl.ds(start, length)] = total[pl.ds(start, length)]
    for stage in reversed(range(len(stages))):
        axis, partner, _ = partners[stage]
        keep, length = spans[stage]
        copy = pltpu.make_async_remote_copy(
            src_ref=sum_ref.at[pl.ds(keep, length)],
            dst_ref=sum_ref.at[pl.ds(keep, length)],
            send_sem=send_sem.at[len(stages) + stage],
            recv_sem=recv_sem.at[len(stages) + stage],
            device_id={axis: partner},
            device_id_type=pl.DeviceIdType.MESH,
        )
        copy.start()
        copy.wait()


def summed(parts):
    stages = []
    for axis in ("col", "row"):
        count = lax.axis_size(axis)
        if count & (count - 1):
            return lax.psum(parts, ("row", "col"))
        stages += [(axis, bit) for bit in range(count.bit_length() - 1)]
    flat = parts.reshape(-1, parts.shape[-1])
    if flat.shape[0] % (8 << len(stages)) or not stages:
        return lax.psum(parts, ("row", "col"))
    total = pl.pallas_call(
        functools.partial(sum_kernel, stages),
        out_shape=jax.ShapeDtypeStruct(flat.shape, F32),
        in_specs=[pl.BlockSpec(memory_space=pltpu.VMEM)],
        out_specs=pl.BlockSpec(memory_space=pltpu.VMEM),
        scratch_shapes=[
            pltpu.VMEM(flat.shape, F32),
            pltpu.VMEM(flat.shape, F32),
            pltpu.SemaphoreType.DMA((2 * len(stages),)),
            pltpu.SemaphoreType.DMA((2 * len(stages),)),
        ],
        compiler_params=pltpu.CompilerParams(collective_id=0, has_side_effects=True),
    )(flat)
    return total.reshape(parts.shape)


def per_device_blocks(
    ancestor_inverse, factor_panels, diag_inverse, coupling, block_pattern, tree_order
):
    grid_row = lax.axis_index("row")
    grid_col = lax.axis_index("col")
    row_count = lax.axis_size("row")
    col_count = lax.axis_size("col")
    size = factor_panels.shape[3]
    tile_blocks = ancestor_inverse.shape[1] // size
    half_blocks = ancestor_inverse.shape[2] // size
    piece_blocks = factor_panels.shape[2] // size
    most = 4 * piece_blocks
    pattern = jnp.take(block_pattern, tree_order, axis=0) > 0
    pattern = jnp.concatenate([pattern[:2], pattern[2:] & pattern[:2]], axis=0)
    pattern = pattern.astype(jnp.int32)
    pieces = pattern.reshape(4, col_count, row_count, piece_blocks).transpose(1, 2, 0, 3)
    flat = pieces.reshape(col_count, row_count, most)
    position = (jnp.cumsum(flat, axis=2) - flat).reshape(pieces.shape)
    counts = jnp.sum(flat, axis=2)
    largest = jnp.max(counts)
    own_flat = flat[grid_col, grid_row]
    own_list = jnp.argsort(1 - own_flat, stable=True).astype(jnp.int32)
    supernode = jnp.take(tree_order, own_list // piece_blocks)
    block = own_list % piece_blocks
    half_live = lax.dynamic_slice_in_dim(pattern, grid_col * half_blocks, half_blocks, 1)
    live_rows = lax.dynamic_slice_in_dim(pattern, grid_row * tile_blocks, tile_blocks, 1)
    half_position = position[grid_col].transpose(1, 0, 2).reshape(4, half_blocks)
    k_source = jnp.arange(half_blocks, dtype=jnp.int32) // piece_blocks
    k_order = jnp.argsort(1 - half_live, axis=1, stable=True).astype(jnp.int32)
    k_live = jnp.sum(half_live, axis=1)
    k_count = (k_live + GROUP - 1) // GROUP
    padded = -(-half_blocks // GROUP) * GROUP
    k_order = jnp.pad(k_order, ((0, 0), (0, padded - half_blocks)))
    inside = jnp.arange(padded, dtype=jnp.int32)[None, :] < k_live[:, None]
    k_list = jnp.where(inside, k_order, k_order[:, :1])
    k_any = jnp.max(half_live, axis=0)
    tile_at = grid_row * tile_blocks + jnp.arange(tile_blocks, dtype=jnp.int32)
    own = (tile_at // half_blocks == grid_col).astype(jnp.int32)
    local = tile_at % half_blocks
    window_source = jnp.stack(
        [
            jnp.broadcast_to((local // piece_blocks)[None, :], (4, tile_blocks)),
            jnp.take(half_position, local, axis=1),
        ]
    ).astype(jnp.int32)

    packed = pack(factor_panels, supernode, block, size)
    least = (most + 1) // 2
    step = max(1, (most - least) // 12)
    sizes = sorted({*range(least, most, step), most})

    def branch(at):
        return lambda blocks: gather_rows(blocks, sizes[at], at)

    choice = jnp.sum((largest > jnp.array(sizes[:-1])).astype(jnp.int32))
    gathered = lax.switch(choice, [branch(at) for at in range(len(sizes))], packed)
    place = jnp.take_along_axis(k_source[None, :] * most + half_position, k_list, axis=1)
    place = jnp.where(inside, place, row_count * most).astype(jnp.int32)
    mine = products_of(
        ancestor_inverse, gathered, counts[grid_col], k_list, place, k_count, live_rows, k_any, size
    )
    other = swapped(mine, "col", 0)
    window_source = jnp.minimum(
        window_source, jnp.array([row_count, most], jnp.int32)[:, None, None] - 1
    )
    inverse_panels, sums = finish(
        mine, other, coupling, gathered, live_rows, own, tree_order, window_source, size
    )
    totals = summed(sums)
    diag_blocks = jnp.take(diag_inverse, tree_order, axis=0)
    parent_diag = [diag_blocks[tree] - totals[tree] for tree in range(2)]
    crosses = [
        -(totals[2 + tree] + multiply(parent_diag[tree], coupling[tree])) for tree in range(2)
    ]
    child_diag = [
        diag_blocks[tree + 2] - totals[4 + tree] - multiply(flipped(coupling[tree]), crosses[tree])
        for tree in range(2)
    ]
    all_diag = jnp.stack(parent_diag + child_diag)
    inverse_diagonal = jnp.take(all_diag, jnp.argsort(tree_order), axis=0)
    return (inverse_panels, inverse_diagonal, jnp.stack(crosses))


def per_device(ancestor_inverse, factor_panels, diag_inverse, coupling, block_pattern, tree_order):
    size = factor_panels.shape[3]
    whole_blocks = math.gcd(ancestor_inverse.shape[1], factor_panels.shape[2]) % size == 0
    run = per_device_blocks if whole_blocks and size % 128 == 0 else per_device_dense
    return run(ancestor_inverse, factor_panels, diag_inverse, coupling, block_pattern, tree_order)


def solution(mesh):
    return jax.shard_map(
        per_device,
        mesh=mesh,
        in_specs=(
            P(None, ("pole", "row"), "col"),
            P(None, None, ("pole", "col", "row"), None),
            P("pole", None, None, None),
            P("pole", None, None, None),
            P(),
            P(),
        ),
        out_specs=(
            P(None, None, ("pole", "row"), None),
            P("pole", None, None, None),
            P("pole", None, None, None),
        ),
        check_vma=False,
    )
```
